32 devices in a mesh: groups: 2 (over x), seq: 16 (over z, y, core).
Axes of the slice: x: 2, y: 2, z: 4, core: 2. Of those that a mesh axis runs over, the one named last changes fastest.
Arguments:
- hidden_states: bfloat16 [37, 512, 2560], P(None, ('groups', 'seq')), parts along dimension 1, may hold values from -80 to 80
- layer_mix: float32 [37], replicated, may hold values from 0.05 to 1
- norm_gain: float32 [2560], replicated, may hold values from 0.1 to 1.9
- norm_bias: float32 [2560], replicated, may hold values from -3 to 3
- proj_in: bfloat16 [2560, 1024], replicated, may hold values from -0.125 to 0.125
- proj_in_bias: float32 [1024], replicated, may hold values from -3 to 3
- proj_out: bfloat16 [1024, 1024], replicated, may hold values from -0.1875 to 0.1875
- proj_out_bias: float32 [1024], replicated, may hold values from -3 to 3
- residue_tokens: int32 [512], P(('groups', 'seq')), parts along dimension 0, may hold values from 0 to 22
- residue_table: float32 [23, 1024], replicated, may hold values from -5 to 5
- pair_norm_gain: float32 [1024], replicated, may hold values from 0.1 to 1.9
- pair_norm_bias: float32 [1024], replicated, may hold values from -3 to 3
- qk_weight: bfloat16 [1024, 128], replicated, may hold values from -0.1875 to 0.1875
- qk_bias: float32 [128], replicated, may hold values from -3 to 3
- pair_weight: bfloat16 [128, 128], replicated, may hold values from -0.75 to 0.75
- relpos_bins: int32 [512, 256], P(('groups', 'seq')), parts along dimension 0, may hold values from 0 to 65
- relpos_table: float32 [66, 128], replicated, may hold values from -5 to 5
- chain_ids: int32 [512], P(('groups', 'seq')), parts along dimension 0, may hold values from 0 to 7, never falling along the last dimension, each value on 1 to 64 neighbouring positions
- chain_table: float32 [2, 128], replicated, may hold values from -5 to 5
Outputs:
- single: bfloat16 [512, 1024], P(('groups', 'seq')), parts along dimension 0
- pair: bfloat16 [512, 256, 128], P(('groups', 'seq')), parts along dimension 0
The draws below stay inside these ranges and needn't reach their ends.
There are 2 independent parts, one for each index of `groups`. The reference program is written for one: setup_inputs(seed, part) draws one part's arguments, and reference() takes and returns one part's arrays. A program takes and returns all parts, laid end to end along the dimension named above; an argument that names none is the same for every part. Nothing has to cross between parts.
Inputs may be any that keep to these rules, and one draw needn't show every extreme that they name: `chain_ids`: chain numbers never fall along the residues; each chain has at most 64 residues.
All inputs are finite; a program needn't handle non-finite values.
Results may differ from the reference program's by a relative error of at most 0.0067.
Values may be sent and summed in bfloat16 or wider, within the bound.
A program may use at most 64 MiB of HBM per device.

```python
import math
import jax
import jax.numpy as jnp
import numpy as np
from jax import lax

D = 2560
CS = 1024
CZ = 128
INNER = 64
NBINS = 66
NAA = 23
NST = 37
NCHAIN = 8
TOK_DEV = 16
L = 256
N_SEQ = 16


def draw_hidden_states(key, part):
    first, second, third = jax.random.split(jax.random.fold_in(key, 11), 3)
    base = jnp.clip(jax.random.normal(first, (NST, L, D), jnp.float32), -4.0, 4.0)
    highest = math.log(10.0)
    col_scale = jnp.exp(jax.random.uniform(second, (NST, 1, D), jnp.float32, 0.0, highest))
    row_scale = jnp.exp(jax.random.uniform(third, (NST, L, 1), jnp.float32, 0.0, highest))
    return (base * col_scale * row_scale * 0.1).astype(jnp.bfloat16)


def touch_ends(array, own_key, low, high):
    shape = array.shape
    spot = [jax.random.randint(jax.random.fold_in(own_key, axis), (), 0, shape[axis]) for axis in range(len(shape))]
    array = array.at[tuple(spot)].set(low)
    longest = shape.index(max(shape))
    spot[longest] = (spot[longest] + 1) % shape[longest]
    return array.at[tuple(spot)].set(high)


def split_up(number_of, total, limit, slope):
    portions = [(1 << 20) // math.isqrt(grade ** slope) + 1 for grade in range(2, number_of + 1)]
    rest, given = total - limit - (number_of - 1), [1] * (number_of - 1)
    while rest > 0:
        movable = [i for i in range(number_of - 1) if given[i] < limit]
        pool, remaining = sum([portions[i] for i in movable]), rest
        for i in movable:
            addition = min(limit - given[i], max(1, remaining * portions[i] // pool), rest)
            given[i] = given[i] + addition
            rest = rest - addition
    return np.array([limit] + given)


def ragged_sizes(stream_key, count, total, limit, lean):
    if count == 2:
        one = jax.random.randint(stream_key, (), max(1, total - limit), min(limit, total - 1) + 1)
        return jnp.stack([one, total - one])
    tallies = jnp.asarray(split_up(count, total, limit, lean), jnp.int32)
    twos = (count - 1) // 2
    source_of, receiver = tallies[1:1 + 2 * twos:2], tallies[2:2 + 2 * twos:2]
    slack = jnp.minimum(source_of - 1, limit - receiver)
    passed = jax.random.randint(jax.random.fold_in(stream_key, 1), (twos,), 0, 1 << 20) % (slack + 1)
    tallies = tallies.at[1:1 + 2 * twos:2].set(source_of - passed).at[2:2 + 2 * twos:2].set(receiver + passed)
    return tallies[jax.random.permutation(jax.random.fold_in(stream_key, 2), count)]


def noise(own_key, shape, scale, bound, held_as=jnp.bfloat16):
    return jnp.clip(scale * jax.random.normal(own_key, shape, jnp.float32), -bound, bound).astype(held_as)


def setup_inputs(seed: int = 0, part: int = 0) -> dict:
    splits = jax.random.split(jax.random.key(seed), 20)
    part_keys = jax.random.split(jax.random.fold_in(splits[19], part), 20)
    hidden_states = draw_hidden_states(jax.random.fold_in(jax.random.fold_in(splits[19], part), 71), part)
    layer_mix = jnp.clip(jnp.exp(jax.random.uniform(splits[1], (NST,), jnp.float32, math.log(0.05), math.log(1.0))), 0.05, 1.0)
    norm_gain = jnp.clip(1.0 + 0.18 * jax.random.normal(splits[2], (D,), jnp.float32), 0.1, 1.9)
    norm_bias = noise(splits[3], (D,), 0.5, 3.0, jnp.float32)
    proj_in = noise(splits[4], (D, CS), D ** -0.5, 0.125)
    proj_in_bias = noise(splits[5], (CS,), 0.5, 3.0, jnp.float32)
    proj_out = noise(splits[6], (CS, CS), CS ** -0.5, 0.1875)
    proj_out_bias = noise(splits[7], (CS,), 0.5, 3.0, jnp.float32)
    residue_tokens = touch_ends(jax.random.randint(part_keys[8], (L,), 0, NAA), jax.random.fold_in(part_keys[8], 1), 0, NAA - 1).astype(jnp.int32)
    residue_table = noise(splits[9], (NAA, CS), 1.0, 5.0, jnp.float32)
    pair_norm_gain = jnp.clip(1.0 + 0.18 * jax.random.normal(splits[10], (CS,), jnp.float32), 0.1, 1.9)
    pair_norm_bias = noise(splits[11], (CS,), 0.5, 3.0, jnp.float32)
    qk_weight = noise(splits[12], (CS, 2 * INNER), CS ** -0.5, 0.1875)
    qk_bias = noise(splits[13], (2 * INNER,), 0.5, 3.0, jnp.float32)
    pair_weight = noise(splits[14], (2 * INNER, CZ), INNER ** -0.5, 0.75)
    relpos_bins = touch_ends(jax.random.randint(part_keys[15], (L, L), 0, NBINS), jax.random.fold_in(part_keys[15], 1), 0, NBINS - 1).astype(jnp.int32)
    relpos_table = noise(splits[16], (NBINS, CZ), 1.0, 5.0, jnp.float32)
    chain_ids = jnp.searchsorted(jnp.cumsum(ragged_sizes(part_keys[17], NCHAIN, L, L // 4, 1)), jnp.arange(L), side="right").astype(jnp.int32)
    chain_table = noise(splits[18], (2, CZ), 1.0, 5.0, jnp.float32)
    return dict(hidden_states=hidden_states, layer_mix=layer_mix, norm_gain=norm_gain, norm_bias=norm_bias, proj_in=proj_in, proj_in_bias=proj_in_bias, proj_out=proj_out, proj_out_bias=proj_out_bias, residue_tokens=residue_tokens, residue_table=residue_table, pair_norm_gain=pair_norm_gain, pair_norm_bias=pair_norm_bias, qk_weight=qk_weight, qk_bias=qk_bias, pair_weight=pair_weight, relpos_bins=relpos_bins, relpos_table=relpos_table, chain_ids=chain_ids, chain_table=chain_table)


epsilon = 1e-05

def layer_norm(values, weight_gain, weight_bias):
    center = values - lax.optimization_barrier(jnp.mean(values, axis=-1, keepdims=True))
    spread = lax.optimization_barrier(jnp.mean(center * center, axis=-1, keepdims=True))
    return center * lax.rsqrt(spread + epsilon) * weight_gain + weight_bias

def single_path(mixture, norm_gain, norm_bias, proj_in, proj_in_bias, proj_out, proj_out_bias, residue_tokens, residue_table, pair_norm_gain, pair_norm_bias, qk_weight, qk_bias, pair_weight):
    normed = layer_norm(mixture, norm_gain, norm_bias).astype(jnp.bfloat16)
    hidden = jax.nn.relu(jnp.dot(normed, proj_in, preferred_element_type=jnp.float32) + proj_in_bias).astype(jnp.bfloat16)
    onehot = (residue_tokens[:, None] == jnp.arange(residue_table.shape[0], dtype=jnp.int32)[None, :]).astype(jnp.float32)
    residue_term = jnp.dot(onehot, residue_table, precision=lax.Precision.HIGHEST)
    single_f = jnp.dot(hidden, proj_out, preferred_element_type=jnp.float32) + proj_out_bias + residue_term
    pair_in = layer_norm(single_f, pair_norm_gain, pair_norm_bias).astype(jnp.bfloat16)
    query_key = jnp.dot(pair_in, qk_weight, preferred_element_type=jnp.float32) + qk_bias
    inner_dim = pair_weight.shape[0] // 2
    queries = query_key[:, :inner_dim].astype(jnp.bfloat16)
    key_rows = query_key[:, inner_dim:].astype(jnp.bfloat16)
    row_diff = jnp.dot(queries, pair_weight[inner_dim:], preferred_element_type=jnp.float32)
    return (single_f, queries, key_rows, row_diff)

def pair_tile(queries, row_diff, row_chain, key_rows, col_diff, col_chain, bin_block, pair_weight, relpos_table, chain_table):
    inner_dim = queries.shape[1]
    row_count = queries.shape[0]
    col_count = key_rows.shape[0]
    products = (queries[:, None, :].astype(jnp.float32) * key_rows[None, :, :].astype(jnp.float32)).astype(jnp.bfloat16)
    product_term = jnp.dot(products.reshape(row_count * col_count, inner_dim), pair_weight[:inner_dim], preferred_element_type=jnp.float32)
    product_term = product_term.reshape(row_count, col_count, -1)
    onehot = (bin_block[:, :, None] == jnp.arange(relpos_table.shape[0], dtype=jnp.int32)[None, None, :]).astype(jnp.float32)
    relpos = jnp.einsum('ijb,bc->ijc', onehot, relpos_table, precision=lax.Precision.HIGHEST)
    same_chain = (row_chain[:, None] == col_chain[None, :])[:, :, None]
    chain_term = jnp.where(same_chain, chain_table[1][None, None, :], chain_table[0][None, None, :])
    summed = product_term + row_diff[:, None, :] - col_diff[None, :, :] + relpos + chain_term
    return summed.astype(jnp.bfloat16)

def reference(hidden_states, layer_mix, norm_gain, norm_bias, proj_in, proj_in_bias, proj_out, proj_out_bias, residue_tokens, residue_table, pair_norm_gain, pair_norm_bias, qk_weight, qk_bias, pair_weight, relpos_bins, relpos_table, chain_ids, chain_table):
    mixture = lax.optimization_barrier(jnp.sum(layer_mix[:, None, None] * hidden_states.astype(jnp.float32), axis=0))
    single_f, queries, key_rows, row_diff = single_path(mixture, norm_gain, norm_bias, proj_in, proj_in_bias, proj_out, proj_out_bias, residue_tokens, residue_table, pair_norm_gain, pair_norm_bias, qk_weight, qk_bias, pair_weight)
    inner_dim = pair_weight.shape[0] // 2
    col_diff = jnp.dot(key_rows, pair_weight[inner_dim:], preferred_element_type=jnp.float32)
    length = relpos_bins.shape[0]
    blocked = (queries.reshape(N_SEQ, TOK_DEV, -1), row_diff.reshape(N_SEQ, TOK_DEV, -1), chain_ids.reshape(N_SEQ, TOK_DEV), relpos_bins.reshape(N_SEQ, TOK_DEV, length))

    def one_block(blocks):
        return pair_tile(blocks[0], blocks[1], blocks[2], key_rows, col_diff, chain_ids, blocks[3], pair_weight, relpos_table, chain_table)
    pair = lax.map(one_block, blocked)
    return (single_f.astype(jnp.bfloat16), pair.reshape(length, length, -1))
```

```python
import functools

import jax
import jax.numpy as jnp
from jax import lax
from jax.experimental import pallas as pl
from jax.experimental.pallas import tpu as pltpu
from jax.sharding import PartitionSpec as P

epsilon = 1e-05
F32 = jnp.float32
BF16 = jnp.bfloat16
LANES = 128
MESH = pl.DeviceIdType.MESH


def layer_norm(values, weight_gain, weight_bias):
    center = values - jnp.mean(values, axis=-1, keepdims=True)
    spread = jnp.mean(center * center, axis=-1, keepdims=True)
    return center * lax.rsqrt(spread + epsilon) * weight_gain + weight_bias


def split_hi_lo(values):
    hi = values.astype(BF16)
    lo = (values - hi.astype(F32)).astype(BF16)
    return hi, lo


def split_three(values):
    hi = values.astype(BF16)
    rest = values - hi.astype(F32)
    mid = rest.astype(BF16)
    low = (rest - mid.astype(F32)).astype(BF16)
    return jnp.concatenate([hi, mid, low], axis=0)


def sum_three(stacked):
    rows = stacked.shape[0] // 3
    return stacked[:rows] + (stacked[rows : 2 * rows] + stacked[2 * rows :])


def column_of(scalars_ref, count, shape):
    rows = lax.broadcasted_iota(jnp.int32, shape, 0)
    out = jnp.zeros(shape, jnp.int32)
    for i in range(count):
        out = jnp.where(rows == i, scalars_ref[i], out)
    return out


def as_row(tiles):
    return jnp.concatenate([tiles[r : r + 1] for r in range(tiles.shape[0])], axis=1)


def pair_block(keys, q_rows, weight, rows):
    lhs = [jnp.concatenate([keys * q_rows[i : i + 1], keys], axis=1) for i in rows]
    return jnp.dot(jnp.concatenate(lhs, axis=0), weight, preferred_element_type=F32)


def kernel(
    n,
    parts,
    h_chunks,
    k_chunks,
    o_chunks,
    hidden_hbm,
    mix_hbm,
    norm_gain_hbm,
    norm_bias_hbm,
    proj_in_hbm,
    proj_in_bias_hbm,
    proj_out_hbm,
    proj_out_bias_hbm,
    tokens_hbm,
    residue_table_hbm,
    pair_gain_hbm,
    pair_bias_hbm,
    qk_weight_hbm,
    qk_bias_hbm,
    pair_weight_hbm,
    bins_hbm,
    relpos_hbm,
    chain_hbm,
    chain_table_hbm,
    single_ref,
    pair_ref,
    base_ref,
    last_keys_ref,
    q_ref,
    weight_ref,
    hidden_v,
    mix_s,
    norm_v,
    proj_in_v,
    vec_v,
    proj_out_v,
    tokens_s,
    residue_table_v,
    qk_weight_v,
    qk_bias_v,
    pair_weight_v,
    bins_v,
    relpos_v,
    chain_s,
    chain_table_v,
    mixture_v,
    residue_v,
    tables_v,
    base_v,
    keys_v,
    copy_sems,
    send_sem,
    recv_sems,
):
    me = lax.axis_index("seq")
    barrier = pltpu.get_barrier_semaphore()
    nst, tok, d = hidden_v.shape
    inner = pair_weight_v.shape[0] // 2
    length = bins_v.shape[1]
    cz = pair_weight_v.shape[1]
    nbins = relpos_v.shape[0]
    nbins_pad = tables_v.shape[0] // 2
    per = n // parts
    width = per * tok
    first = length - width
    n_sems = [0]

    def fetch(*pairs):
        sem = copy_sems.at[n_sems[0]]
        n_sems[0] += 1
        copies = [pltpu.make_async_copy(src, dst, sem) for src, dst in pairs]
        for copy in copies:
            copy.start()
        return copies[0]

    def whole(ref):
        sem = copy_sems.at[n_sems[0] - 1]
        return pltpu.make_async_copy(ref, ref, sem)

    mix_copy = fetch((mix_hbm, mix_s))
    h_width = d // h_chunks
    h_copies = [
        fetch(
            (
                hidden_hbm.at[:, :, pl.ds(c * h_width, h_width)],
                hidden_v.at[:, :, pl.ds(c * h_width, h_width)],
            )
        )
        for c in range(h_chunks)
    ]
    fetch((norm_gain_hbm, norm_v.at[0]), (norm_bias_hbm, norm_v.at[1]))
    norm_copy = whole(norm_v)
    k_depth = d // k_chunks
    in_copies = [
        fetch(
            (
                proj_in_hbm.at[pl.ds(c * k_depth, k_depth), :],
                proj_in_v.at[pl.ds(c * k_depth, k_depth), :],
            )
        )
        for c in range(k_chunks)
    ]
    tok_copy = fetch((tokens_hbm, tokens_s))
    chain_copy = fetch((chain_hbm, chain_s))
    table_copy = fetch((residue_table_hbm, residue_table_v))
    fetch(
        (proj_in_bias_hbm, vec_v.at[0]),
        (proj_out_bias_hbm, vec_v.at[1]),
        (pair_gain_hbm, vec_v.at[2]),
        (pair_bias_hbm, vec_v.at[3]),
    )
    vec_copy = whole(vec_v)
    qk_copies = [fetch((qk_weight_hbm, qk_weight_v)), fetch((qk_bias_hbm, qk_bias_v))]
    o_depth = proj_out_v.shape[0] // o_chunks
    out_copies = [
        fetch(
            (
                proj_out_hbm.at[pl.ds(c * o_depth, o_depth), :],
                proj_out_v.at[pl.ds(c * o_depth, o_depth), :],
            )
        )
        for c in range(o_chunks)
    ]
    pair_copies = [
        fetch((pair_weight_hbm, pair_weight_v)),
        fetch((bins_hbm, bins_v)),
        fetch((relpos_hbm, relpos_v)),
        fetch((chain_table_hbm, chain_table_v)),
    ]

    for step in range(1, n):
        pl.semaphore_signal(
            barrier,
            inc=1,
            device_id={"seq": lax.rem(me + step, n)},
            device_id_type=MESH,
        )

    mix_copy.wait()
    for c in range(h_chunks):
        h_copies[c].wait()
        cols = pl.ds(c * h_width, h_width)
        total = mix_s[0] * hidden_v[0, :, cols].astype(F32)
        for k in range(1, nst):
            total = total + mix_s[k] * hidden_v[k, :, cols].astype(F32)
        mixture_v[:, cols] = total

    norm_copy.wait()
    normed = layer_norm(mixture_v[...], as_row(norm_v[0]), as_row(norm_v[1])).astype(BF16)

    hidden = jnp.zeros((tok, proj_in_v.shape[1]), F32)
    for c in range(k_chunks):
        in_copies[c].wait()
        hidden = hidden + jnp.dot(
            normed[:, c * k_depth : (c + 1) * k_depth],
            proj_in_v[pl.ds(c * k_depth, k_depth), :],
            preferred_element_type=F32,
        )
    tok_copy.wait()
    chain_copy.wait()
    table_copy.wait()
    for i in range(tok):
        residue_v[pl.ds(i, 1), :] = residue_table_v[pl.ds(tokens_s[i], 1), :]
    vec_copy.wait()
    for copy in qk_copies:
        copy.wait()
    hidden = jnp.maximum(hidden + vec_v[0], 0.0).astype(BF16)
    gain = vec_v[2]
    qk_weight = qk_weight_v[...]
    affine = sum_three(
        jnp.dot(
            split_three(
                jnp.concatenate(
                    [jnp.broadcast_to(gain, (8,) + gain.shape[1:]), jnp.broadcast_to(vec_v[3], (8,) + gain.shape[1:])],
                    axis=0,
                )
            ),
            qk_weight,
            preferred_element_type=F32,
        )
    )
    gain_w = affine[0:1]
    bias_w = affine[8:9] + qk_bias_v[...]
    single_f = vec_v[1] + residue_v[...]
    for c in range(o_chunks):
        out_copies[c].wait()
        single_f = single_f + jnp.dot(
            hidden[:, c * o_depth : (c + 1) * o_depth],
            proj_out_v[pl.ds(c * o_depth, o_depth), :],
            preferred_element_type=F32,
        )
    raw = jnp.dot(split_three(single_f * gain), qk_weight, preferred_element_type=F32)
    mean = jnp.mean(single_f, axis=-1, keepdims=True)
    center = single_f - mean
    scale = lax.rsqrt(jnp.mean(center * center, axis=-1, keepdims=True) + epsilon)
    query_key = (sum_three(raw) - mean * gain_w) * scale + bias_w

    span = (LANES - inner) // 2
    lane = lax.broadcasted_iota(jnp.int32, (tok, LANES), 1)
    chains = column_of(chain_s, tok, (tok, LANES))
    onehot = jnp.where(
        (lane == chains + inner) | (lane == chains + (inner + span)), 1.0, 0.0
    ).astype(F32)
    q_rows = jnp.where(lane < inner, query_key, onehot).astype(BF16)
    keys_v[me] = jnp.where(
        lane < inner, pltpu.roll(query_key, LANES - inner, 1), onehot
    ).astype(BF16)

    pl.semaphore_wait(barrier, n - 1)
    for place in range(n):
        target = jnp.where(2 * me >= n, place, n - 1 - place)

        @pl.when(target != me)
        def _():
            pltpu.make_async_remote_copy(
                src_ref=keys_v.at[me],
                dst_ref=keys_v.at[me],
                send_sem=send_sem,
                recv_sem=recv_sems.at[me // per],
                device_id={"seq": target},
                device_id_type=MESH,
            ).start()

    q_ref[...] = q_rows
    single_ref[...] = single_f.astype(BF16)
    for copy in pair_copies:
        copy.wait()
    pair_weight = pair_weight_v[...]
    low_weight = pair_weight[inner:]
    row_diff = jnp.dot(q_rows[:, :inner], low_weight, preferred_element_type=F32)
    chain_base = chain_table_v[pl.ds(0, 1), :]
    chain_hi, chain_lo = split_hi_lo(chain_table_v[pl.ds(1, 1), :] - chain_base)
    weight = jnp.concatenate(
        [
            pair_weight[:inner],
            jnp.broadcast_to(chain_hi, (span, cz)),
            jnp.broadcast_to(chain_lo, (span, cz)),
            -low_weight,
            jnp.zeros((LANES - inner, cz), BF16),
        ],
        axis=0,
    )
    weight_ref[...] = weight
    tables_v[...] = jnp.zeros_like(tables_v)
    hi, lo = split_hi_lo(relpos_v[...])
    tables_v[pl.ds(0, nbins), :] = hi
    tables_v[pl.ds(nbins_pad, nbins), :] = lo
    tables = tables_v[...]
    row_base = row_diff + chain_base
    bins = jnp.concatenate(
        [bins_v[...], jnp.zeros((LANES - tok, length), jnp.int32)], axis=0
    )
    bins_t = bins.T
    bin_lane = lax.broadcasted_iota(jnp.int32, (length, nbins_pad), 1)
    for i in range(tok):
        hot = jnp.where(bins_t[:, i : i + 1] == bin_lane, 1.0, 0.0).astype(BF16)
        base = (
            jnp.dot(
                jnp.concatenate([hot, hot], axis=1), tables, preferred_element_type=F32
            )
            + row_base[i : i + 1]
        )
        base_v[i] = base[:first]
        base_ref[i] = base[first:]

    def arrived(part, count):
        block = keys_v.at[pl.ds(part * per, count)]
        pltpu.make_async_remote_copy(
            src_ref=block,
            dst_ref=block,
            send_sem=send_sem,
            recv_sem=recv_sems.at[part],
            device_id={"seq": lax.rem(me + 1, n)},
            device_id_type=MESH,
        ).wait_recv()

    for part in range(parts):
        own = me // per == part

        @pl.when(jnp.logical_not(own))
        def _():
            arrived(part, per)

        if per > 1:

            @pl.when(own)
            def _():
                arrived(part, per - 1)

        keys = keys_v[pl.ds(part * per, per)].reshape(width, LANES)
        if part == parts - 1:
            last_keys_ref[...] = keys
        else:
            block = pair_block(keys, q_rows, weight, range(tok))
            for i in range(tok):
                pair_ref[i, pl.ds(part * width, width), :] = (
                    block[i * width : (i + 1) * width]
                    + base_v[i, pl.ds(part * width, width), :]
                ).astype(BF16)
    sent = keys_v.at[pl.ds(0, n - 1)]
    pltpu.make_async_remote_copy(
        src_ref=sent,
        dst_ref=sent,
        send_sem=send_sem,
        recv_sem=recv_sems.at[0],
        device_id={"seq": lax.rem(me + 1, n)},
        device_id_type=MESH,
    ).wait_send()


def finish(
    single_ref, pair_ref, base_ref, keys_ref, q_ref, weight_ref,
    single_hbm, pair_hbm, last_v, sems,
):
    tok, width, cz = base_ref.shape
    first = pair_ref.shape[1]
    copies = []

    def put(src, dst):
        copies.append(pltpu.make_async_copy(src, dst, sems.at[len(copies)]))
        copies[-1].start()

    put(pair_ref, pair_hbm.at[:, pl.ds(0, first), :])
    put(single_ref, single_hbm)
    halves = 2
    rows = tok // halves
    for h in range(halves):
        block = pair_block(
            keys_ref[...], q_ref[...], weight_ref[...], range(h * rows, (h + 1) * rows)
        )
        for i in range(rows):
            last_v[h * rows + i] = (
                block[i * width : (i + 1) * width] + base_ref[h * rows + i]
            ).astype(BF16)
        put(
            last_v.at[pl.ds(h * rows, rows)],
            pair_hbm.at[pl.ds(h * rows, rows), pl.ds(first, width), :],
        )
    for copy in copies:
        copy.wait()


def shards(n, *args):
    (hidden, mix, norm_gain, norm_bias, proj_in, proj_in_bias, proj_out, proj_out_bias,
     tokens, residue_table, pair_gain, pair_bias, qk_weight, qk_bias, pair_weight,
     bins, relpos, chain, chain_table) = args
    row = lambda a: a.reshape(1, a.shape[0])
    tiles = lambda a: a.reshape(a.shape[0] // LANES, LANES)
    args = (hidden, mix, tiles(norm_gain), tiles(norm_bias), proj_in, row(proj_in_bias),
            proj_out, row(proj_out_bias), tokens, residue_table, row(pair_gain),
            row(pair_bias), qk_weight, row(qk_bias), pair_weight, bins, relpos, chain,
            chain_table)
    args = tuple(pltpu.with_memory_space_constraint(a, pltpu.HBM) for a in args)
    nst, tok, d = hidden.shape
    cs = proj_out.shape[1]
    cz = pair_weight.shape[1]
    length = bins.shape[1]
    like = lambda a: pltpu.VMEM(a.shape, a.dtype)
    scalars = lambda a: pltpu.SMEM(a.shape, a.dtype)
    nbins_pad = -(-relpos.shape[0] // LANES) * LANES
    h_chunks = k_chunks = 5 if d % (5 * LANES) == 0 else 1
    o_chunks = 4 if proj_out.shape[0] % (4 * LANES) == 0 else 1
    n_copies = 14 + h_chunks + k_chunks + o_chunks
    parts = 8 if n % 8 == 0 else 2
    width = length // parts
    first = length - width
    vmem = pl.BlockSpec(memory_space=pltpu.VMEM)
    hbm = pl.BlockSpec(memory_space=pltpu.HBM)
    mid = pl.pallas_call(
        functools.partial(kernel, n, parts, h_chunks, k_chunks, o_chunks),
        out_shape=(
            jax.ShapeDtypeStruct((tok, cs), BF16),
            jax.ShapeDtypeStruct((tok, first, cz), BF16),
            jax.ShapeDtypeStruct((tok, width, cz), F32),
            jax.ShapeDtypeStruct((width, LANES), BF16),
            jax.ShapeDtypeStruct((tok, LANES), BF16),
            jax.ShapeDtypeStruct((2 * LANES, cz), BF16),
        ),
        in_specs=[hbm] * len(args),
        out_specs=(vmem,) * 6,
        scratch_shapes=[
            like(hidden),
            scalars(mix),
            pltpu.VMEM((2, d // LANES, LANES), F32),
            like(proj_in),
            pltpu.VMEM((4, 1, cs), F32),
            like(proj_out),
            scalars(tokens),
            like(residue_table),
            like(qk_weight),
            pltpu.VMEM((1, qk_bias.shape[0]), F32),
            like(pair_weight),
            like(bins),
            like(relpos),
            scalars(chain),
            like(chain_table),
            pltpu.VMEM((tok, d), F32),
            pltpu.VMEM((tok, cs), F32),
            pltpu.VMEM((2 * nbins_pad, cz), BF16),
            pltpu.VMEM((tok, first, cz), F32),
            pltpu.VMEM((n, tok, LANES), BF16),
            pltpu.SemaphoreType.DMA((n_copies,)),
            pltpu.SemaphoreType.DMA,
            pltpu.SemaphoreType.DMA((parts,)),
        ],
        compiler_params=pltpu.CompilerParams(
            collective_id=0, has_side_effects=True, vmem_limit_bytes=40 << 20
        ),
    )(*args)
    return pl.pallas_call(
        finish,
        out_shape=(
            jax.ShapeDtypeStruct((tok, cs), BF16),
            jax.ShapeDtypeStruct((tok, length, cz), BF16),
        ),
        in_specs=[vmem] * 6,
        out_specs=(hbm, hbm),
        scratch_shapes=[
            pltpu.VMEM((tok, width, cz), BF16),
            pltpu.SemaphoreType.DMA((4,)),
        ],
        compiler_params=pltpu.CompilerParams(vmem_limit_bytes=16 << 20),
    )(*mid)


def solution(mesh):
    in_specs = (
        P(None, ("groups", "seq"), None),
        P(),
        P(),
        P(),
        P(),
        P(),
        P(),
        P(),
        P(("groups", "seq")),
        P(),
        P(),
        P(),
        P(),
        P(),
        P(),
        P(("groups", "seq"), None),
        P(),
        P(("groups", "seq")),
        P(),
    )
    out_specs = (P(("groups", "seq"), None), P(("groups", "seq"), None, None))
    return jax.shard_map(
        functools.partial(shards, mesh.shape["seq"]),
        mesh=mesh,
        in_specs=in_specs,
        out_specs=out_specs,
        check_vma=False,
    )
```

```python
import functools

import jax
import jax.numpy as jnp
from jax import lax
from jax.experimental import pallas as pl
from jax.experimental.pallas import tpu as pltpu
from jax.sharding import PartitionSpec as P

epsilon = 1e-05
F32 = jnp.float32
BF16 = jnp.bfloat16
LANES = 128
MESH = pl.DeviceIdType.MESH


def layer_norm(values, weight_gain, weight_bias):
    center = values - jnp.mean(values, axis=-1, keepdims=True)
    spread = jnp.mean(center * center, axis=-1, keepdims=True)
    return center * lax.rsqrt(spread + epsilon) * weight_gain + weight_bias


def split_hi_lo(values):
    hi = values.astype(BF16)
    lo = (values - hi.astype(F32)).astype(BF16)
    return hi, lo


def split_three(values):
    hi = values.astype(BF16)
    rest = values - hi.astype(F32)
    mid = rest.astype(BF16)
    low = (rest - mid.astype(F32)).astype(BF16)
    return jnp.concatenate([hi, mid, low], axis=0)


def sum_three(stacked):
    rows = stacked.shape[0] // 3
    return stacked[:rows] + (stacked[rows : 2 * rows] + stacked[2 * rows :])


def column_of(scalars_ref, count, shape):
    rows = lax.broadcasted_iota(jnp.int32, shape, 0)
    out = jnp.zeros(shape, jnp.int32)
    for i in range(count):
        out = jnp.where(rows == i, scalars_ref[i], out)
    return out


def as_row(tiles):
    return jnp.concatenate([tiles[r : r + 1] for r in range(tiles.shape[0])], axis=1)


def pair_block(keys, q_rows, weight, rows):
    lhs = [jnp.concatenate([keys * q_rows[i : i + 1], keys], axis=1) for i in rows]
    return jnp.dot(jnp.concatenate(lhs, axis=0), weight, preferred_element_type=F32)


def kernel(
    n,
    parts,
    h_chunks,
    k_chunks,
    o_chunks,
    n_copies,
    hidden_hbm,
    mix_hbm,
    norm_gain_hbm,
    norm_bias_hbm,
    proj_in_hbm,
    proj_in_bias_hbm,
    proj_out_hbm,
    proj_out_bias_hbm,
    tokens_hbm,
    residue_table_hbm,
    pair_gain_hbm,
    pair_bias_hbm,
    qk_weight_hbm,
    qk_bias_hbm,
    pair_weight_hbm,
    bins_hbm,
    relpos_hbm,
    chain_hbm,
    chain_table_hbm,
    single_ref,
    pair_ref,
    base_ref,
    last_keys_ref,
    q_ref,
    weight_ref,
    hidden_v,
    mix_s,
    norm_v,
    proj_in_v,
    vec_v,
    proj_out_v,
    tokens_s,
    residue_table_v,
    qk_weight_v,
    qk_bias_v,
    pair_weight_v,
    bins_v,
    relpos_v,
    chain_s,
    chain_table_v,
    mixture_v,
    residue_v,
    tables_v,
    base_v,
    keys_v,
    send_sem,
    recv_sems,
):
    me = lax.axis_index("seq")
    barrier = pltpu.get_barrier_semaphore()
    nst, tok, d = hidden_v.shape
    inner = pair_weight_v.shape[0] // 2
    length = bins_v.shape[1]
    cz = pair_weight_v.shape[1]
    nbins = relpos_v.shape[0]
    nbins_pad = tables_v.shape[0] // 2
    per = n // parts
    width = per * tok
    first = length - width
    def produce(copy_sems):
        n_sems = [0]

        def fetch(*pairs):
            sem = copy_sems.at[n_sems[0]]
            n_sems[0] += 1
            copies = [pltpu.make_async_copy(src, dst, sem) for src, dst in pairs]
            for copy in copies:
                copy.start()
            return copies[0]

        def whole(ref):
            sem = copy_sems.at[n_sems[0] - 1]
            return pltpu.make_async_copy(ref, ref, sem)

        mix_copy = fetch((mix_hbm, mix_s))
        h_width = d // h_chunks
        h_copies = [
            fetch(
                (
                    hidden_hbm.at[:, :, pl.ds(c * h_width, h_width)],
                    hidden_v.at[:, :, pl.ds(c * h_width, h_width)],
                )
            )
            for c in range(h_chunks)
        ]
        fetch((norm_gain_hbm, norm_v.at[0]), (norm_bias_hbm, norm_v.at[1]))
        norm_copy = whole(norm_v)
        k_depth = d // k_chunks
        tok_copy = fetch((tokens_hbm, tokens_s))
        chain_copy = fetch((chain_hbm, chain_s))
        table_copy = fetch((residue_table_hbm, residue_table_v))
        fetch(
            (proj_in_bias_hbm, vec_v.at[0]),
            (proj_out_bias_hbm, vec_v.at[1]),
            (pair_gain_hbm, vec_v.at[2]),
            (pair_bias_hbm, vec_v.at[3]),
        )
        vec_copy = whole(vec_v)
        qk_copies = [fetch((qk_weight_hbm, qk_weight_v)), fetch((qk_bias_hbm, qk_bias_v))]
        in_copies = [
            fetch(
                (
                    proj_in_hbm.at[pl.ds(c * k_depth, k_depth), :],
                    proj_in_v.at[pl.ds(c * k_depth, k_depth), :],
                )
            )
            for c in range(k_chunks)
        ]
        o_depth = proj_out_v.shape[0] // o_chunks
        out_copies = [
            fetch(
                (
                    proj_out_hbm.at[pl.ds(c * o_depth, o_depth), :],
                    proj_out_v.at[pl.ds(c * o_depth, o_depth), :],
                )
            )
            for c in range(o_chunks)
        ]

        for step in range(1, n):
            pl.semaphore_signal(
                barrier,
                inc=1,
                device_id={"seq": lax.rem(me + step, n)},
                device_id_type=MESH,
            )

        mix_copy.wait()
        for c in range(h_chunks):
            h_copies[c].wait()
            cols = pl.ds(c * h_width, h_width)
            total = mix_s[0] * hidden_v[0, :, cols].astype(F32)
            for k in range(1, nst):
                total = total + mix_s[k] * hidden_v[k, :, cols].astype(F32)
            mixture_v[:, cols] = total

        norm_copy.wait()
        normed = layer_norm(mixture_v[...], as_row(norm_v[0]), as_row(norm_v[1])).astype(BF16)

        hidden = jnp.zeros((tok, proj_in_v.shape[1]), F32)
        for c in range(k_chunks):
            in_copies[c].wait()
            hidden = hidden + jnp.dot(
                normed[:, c * k_depth : (c + 1) * k_depth],
                proj_in_v[pl.ds(c * k_depth, k_depth), :],
                preferred_element_type=F32,
            )
            if c == 0:
                tok_copy.wait()
                chain_copy.wait()
                table_copy.wait()
                for i in range(tok):
                    residue_v[pl.ds(i, 1), :] = residue_table_v[pl.ds(tokens_s[i], 1), :]
                span = (LANES - inner) // 2
                lane = lax.broadcasted_iota(jnp.int32, (tok, LANES), 1)
                chains = column_of(chain_s, tok, (tok, LANES))
                onehot = jnp.where(
                    (lane == chains + inner) | (lane == chains + (inner + span)), 1.0, 0.0
                ).astype(F32)
            if c == min(1, k_chunks - 1):
                vec_copy.wait()
                for copy in qk_copies:
                    copy.wait()
                gain = vec_v[2]
                qk_weight = qk_weight_v[...]
                affine = sum_three(
                    jnp.dot(
                        split_three(
                            jnp.concatenate(
                                [jnp.broadcast_to(gain, (8,) + gain.shape[1:]), jnp.broadcast_to(vec_v[3], (8,) + gain.shape[1:])],
                                axis=0,
                            )
                        ),
                        qk_weight,
                        preferred_element_type=F32,
                    )
                )
                gain_w = affine[0:1]
                bias_w = affine[8:9] + qk_bias_v[...]
        hidden = jnp.maximum(hidden + vec_v[0], 0.0).astype(BF16)
        single_f = vec_v[1] + residue_v[...]
        for c in range(o_chunks):
            out_copies[c].wait()
            single_f = single_f + jnp.dot(
                hidden[:, c * o_depth : (c + 1) * o_depth],
                proj_out_v[pl.ds(c * o_depth, o_depth), :],
                preferred_element_type=F32,
            )
        raw = jnp.dot(split_three(single_f * gain), qk_weight, preferred_element_type=F32)
        mean = jnp.mean(single_f, axis=-1, keepdims=True)
        center = single_f - mean
        scale = lax.rsqrt(jnp.mean(center * center, axis=-1, keepdims=True) + epsilon)
        query_key = (sum_three(raw) - mean * gain_w) * scale + bias_w

        q_rows = jnp.where(lane < inner, query_key, onehot).astype(BF16)
        keys_v[me] = jnp.where(
            lane < inner, pltpu.roll(query_key, LANES - inner, 1), onehot
        ).astype(BF16)

        pl.semaphore_wait(barrier, n - 1)
        for place in range(n):
            target = jnp.where(2 * me >= n, place, n - 1 - place)

            @pl.when(target != me)
            def _():
                pltpu.make_async_remote_copy(
                    src_ref=keys_v.at[me],
                    dst_ref=keys_v.at[me],
                    send_sem=send_sem,
                    recv_sem=recv_sems.at[me // per],
                    device_id={"seq": target},
                    device_id_type=MESH,
                ).start()

        pair_copies = [
            fetch((pair_weight_hbm, pair_weight_v)),
            fetch((bins_hbm, bins_v)),
            fetch((relpos_hbm, relpos_v)),
            fetch((chain_table_hbm, chain_table_v)),
        ]
        q_ref[...] = q_rows
        single_ref[...] = single_f.astype(BF16)
        for copy in pair_copies:
            copy.wait()
        pair_weight = pair_weight_v[...]
        low_weight = pair_weight[inner:]
        row_diff = jnp.dot(q_rows[:, :inner], low_weight, preferred_element_type=F32)
        chain_base = chain_table_v[pl.ds(0, 1), :]
        chain_hi, chain_lo = split_hi_lo(chain_table_v[pl.ds(1, 1), :] - chain_base)
        weight = jnp.concatenate(
            [
                pair_weight[:inner],
                jnp.broadcast_to(chain_hi, (span, cz)),
                jnp.broadcast_to(chain_lo, (span, cz)),
                -low_weight,
                jnp.zeros((LANES - inner, cz), BF16),
            ],
            axis=0,
        )
        weight_ref[...] = weight
        tables_v[...] = jnp.zeros_like(tables_v)
        hi, lo = split_hi_lo(relpos_v[...])
        tables_v[pl.ds(0, nbins), :] = hi
        tables_v[pl.ds(nbins_pad, nbins), :] = lo
        tables = tables_v[...]
        row_base = row_diff + chain_base
        bins = jnp.concatenate(
            [bins_v[...], jnp.zeros((LANES - tok, length), jnp.int32)], axis=0
        )
        bins_t = bins.T
        bin_lane = lax.broadcasted_iota(jnp.int32, (length, nbins_pad), 1)
        for i in range(tok):
            hot = jnp.where(bins_t[:, i : i + 1] == bin_lane, 1.0, 0.0).astype(BF16)
            base = (
                jnp.dot(
                    jnp.concatenate([hot, hot], axis=1), tables, preferred_element_type=F32
                )
                + row_base[i : i + 1]
            )
            base_v[i] = base[:first]
            base_ref[i] = base[first:]

    pl.run_scoped(produce, pltpu.SemaphoreType.DMA((n_copies,)))
    q_rows = q_ref[...]
    weight = weight_ref[...]

    def arrived(part, count):
        block = keys_v.at[pl.ds(part * per, count)]
        pltpu.make_async_remote_copy(
            src_ref=block,
            dst_ref=block,
            send_sem=send_sem,
            recv_sem=recv_sems.at[part],
            device_id={"seq": lax.rem(me + 1, n)},
            device_id_type=MESH,
        ).wait_recv()

    for part in range(parts):
        own = me // per == part

        @pl.when(jnp.logical_not(own))
        def _():
            arrived(part, per)

        if per > 1:

            @pl.when(own)
            def _():
                arrived(part, per - 1)

        keys = keys_v[pl.ds(part * per, per)].reshape(width, LANES)
        if part == parts - 1:
            last_keys_ref[...] = keys
        else:
            block = pair_block(keys, q_rows, weight, range(tok))
            for i in range(tok):
                pair_ref[i, pl.ds(part * width, width), :] = (
                    block[i * width : (i + 1) * width]
                    + base_v[i, pl.ds(part * width, width), :]
                ).astype(BF16)
    sent = keys_v.at[pl.ds(0, n - 1)]
    pltpu.make_async_remote_copy(
        src_ref=sent,
        dst_ref=sent,
        send_sem=send_sem,
        recv_sem=recv_sems.at[0],
        device_id={"seq": lax.rem(me + 1, n)},
        device_id_type=MESH,
    ).wait_send()


def finish(
    single_ref, pair_ref, base_ref, keys_ref, q_ref, weight_ref,
    single_hbm, pair_hbm, last_v, sems,
):
    tok, width, cz = base_ref.shape
    first = pair_ref.shape[1]
    copies = []

    def put(src, dst):
        copies.append(pltpu.make_async_copy(src, dst, sems.at[len(copies)]))
        copies[-1].start()

    put(pair_ref, pair_hbm.at[:, pl.ds(0, first), :])
    put(single_ref, single_hbm)
    halves = 2
    rows = tok // halves
    for h in range(halves):
        block = pair_block(
            keys_ref[...], q_ref[...], weight_ref[...], range(h * rows, (h + 1) * rows)
        )
        for i in range(rows):
            last_v[h * rows + i] = (
                block[i * width : (i + 1) * width] + base_ref[h * rows + i]
            ).astype(BF16)
        put(
            last_v.at[pl.ds(h * rows, rows)],
            pair_hbm.at[pl.ds(h * rows, rows), pl.ds(first, width), :],
        )
    for copy in copies:
        copy.wait()


def shards(n, *args):
    (hidden, mix, norm_gain, norm_bias, proj_in, proj_in_bias, proj_out, proj_out_bias,
     tokens, residue_table, pair_gain, pair_bias, qk_weight, qk_bias, pair_weight,
     bins, relpos, chain, chain_table) = args
    row = lambda a: a.reshape(1, a.shape[0])
    tiles = lambda a: a.reshape(a.shape[0] // LANES, LANES)
    args = (hidden, mix, tiles(norm_gain), tiles(norm_bias), proj_in, row(proj_in_bias),
            proj_out, row(proj_out_bias), tokens, residue_table, row(pair_gain),
            row(pair_bias), qk_weight, row(qk_bias), pair_weight, bins, relpos, chain,
            chain_table)
    args = tuple(pltpu.with_memory_space_constraint(a, pltpu.HBM) for a in args)
    nst, tok, d = hidden.shape
    cs = proj_out.shape[1]
    cz = pair_weight.shape[1]
    length = bins.shape[1]
    like = lambda a: pltpu.VMEM(a.shape, a.dtype)
    scalars = lambda a: pltpu.SMEM(a.shape, a.dtype)
    nbins_pad = -(-relpos.shape[0] // LANES) * LANES
    h_chunks, k_chunks = (5, 10) if d % (10 * LANES) == 0 else (1, 1)
    o_chunks = 4 if proj_out.shape[0] % (4 * LANES) == 0 else 1
    n_copies = 14 + h_chunks + k_chunks + o_chunks
    parts = 8 if n % 8 == 0 else 2
    width = length // parts
    first = length - width
    vmem = pl.BlockSpec(memory_space=pltpu.VMEM)
    hbm = pl.BlockSpec(memory_space=pltpu.HBM)
    mid = pl.pallas_call(
        functools.partial(kernel, n, parts, h_chunks, k_chunks, o_chunks, n_copies),
        out_shape=(
            jax.ShapeDtypeStruct((tok, cs), BF16),
            jax.ShapeDtypeStruct((tok, first, cz), BF16),
            jax.ShapeDtypeStruct((tok, width, cz), F32),
            jax.ShapeDtypeStruct((width, LANES), BF16),
            jax.ShapeDtypeStruct((tok, LANES), BF16),
            jax.ShapeDtypeStruct((2 * LANES, cz), BF16),
        ),
        in_specs=[hbm] * len(args),
        out_specs=(vmem,) * 6,
        scratch_shapes=[
            like(hidden),
            scalars(mix),
            pltpu.VMEM((2, d // LANES, LANES), F32),
            like(proj_in),
            pltpu.VMEM((4, 1, cs), F32),
            like(proj_out),
            scalars(tokens),
            like(residue_table),
            like(qk_weight),
            pltpu.VMEM((1, qk_bias.shape[0]), F32),
            like(pair_weight),
            like(bins),
            like(relpos),
            scalars(chain),
            like(chain_table),
            pltpu.VMEM((tok, d), F32),
            pltpu.VMEM((tok, cs), F32),
            pltpu.VMEM((2 * nbins_pad, cz), BF16),
            pltpu.VMEM((tok, first, cz), F32),
            pltpu.VMEM((n, tok, LANES), BF16),
            pltpu.SemaphoreType.DMA,
            pltpu.SemaphoreType.DMA((parts,)),
        ],
        compiler_params=pltpu.CompilerParams(
            collective_id=0, has_side_effects=True, vmem_limit_bytes=40 << 20
        ),
    )(*args)
    return pl.pallas_call(
        finish,
        out_shape=(
            jax.ShapeDtypeStruct((tok, cs), BF16),
            jax.ShapeDtypeStruct((tok, length, cz), BF16),
        ),
        in_specs=[vmem] * 6,
        out_specs=(hbm, hbm),
        scratch_shapes=[
            pltpu.VMEM((tok, width, cz), BF16),
            pltpu.SemaphoreType.DMA((4,)),
        ],
        compiler_params=pltpu.CompilerParams(vmem_limit_bytes=16 << 20),
    )(*mid)


def solution(mesh):
    in_specs = (
        P(None, ("groups", "seq"), None),
        P(),
        P(),
        P(),
        P(),
        P(),
        P(),
        P(),
        P(("groups", "seq")),
        P(),
        P(),
        P(),
        P(),
        P(),
        P(),
        P(("groups", "seq"), None),
        P(),
        P(("groups", "seq")),
        P(),
    )
    out_specs = (P(("groups", "seq"), None), P(("groups", "seq"), None, None))
    return jax.shard_map(
        functools.partial(shards, mesh.shape["seq"]),
        mesh=mesh,
        in_specs=in_specs,
        out_specs=out_specs,
        check_vma=False,
    )
```

```python
import functools

import jax
import jax.numpy as jnp
from jax import lax
from jax.experimental import pallas as pl
from jax.experimental.pallas import tpu as pltpu
from jax.sharding import PartitionSpec as P

epsilon = 1e-05
F32 = jnp.float32
BF16 = jnp.bfloat16
LANES = 128
MESH = pl.DeviceIdType.MESH


def layer_norm(values, weight_gain, weight_bias):
    center = values - jnp.mean(values, axis=-1, keepdims=True)
    spread = jnp.mean(center * center, axis=-1, keepdims=True)
    return center * lax.rsqrt(spread + epsilon) * weight_gain + weight_bias


def split_hi_lo(values):
    hi = values.astype(BF16)
    lo = (values - hi.astype(F32)).astype(BF16)
    return hi, lo


def split_three(values):
    hi = values.astype(BF16)
    rest = values - hi.astype(F32)
    mid = rest.astype(BF16)
    low = (rest - mid.astype(F32)).astype(BF16)
    return jnp.concatenate([hi, mid, low], axis=0)


def split_rows(values):
    return jnp.concatenate(split_hi_lo(values), axis=0)


def sum_three(stacked):
    rows = stacked.shape[0] // 3
    return stacked[:rows] + (stacked[rows : 2 * rows] + stacked[2 * rows :])


def column_of(scalars_ref, count, shape):
    rows = lax.broadcasted_iota(jnp.int32, shape, 0)
    out = jnp.zeros(shape, jnp.int32)
    for i in range(count):
        out = jnp.where(rows == i, scalars_ref[i], out)
    return out


def as_row(tiles):
    return jnp.concatenate([tiles[r : r + 1] for r in range(tiles.shape[0])], axis=1)


def pair_block(keys, q_rows, weight, rows):
    lhs = [jnp.concatenate([keys * q_rows[i : i + 1], keys], axis=1) for i in rows]
    return jnp.dot(jnp.concatenate(lhs, axis=0), weight, preferred_element_type=F32)


def kernel(
    n,
    parts,
    h_chunks,
    k_chunks,
    o_chunks,
    n_copies,
    hidden_hbm,
    mix_hbm,
    norm_gain_hbm,
    norm_bias_hbm,
    proj_in_hbm,
    proj_in_bias_hbm,
    proj_out_hbm,
    proj_out_bias_hbm,
    tokens_hbm,
    residue_table_hbm,
    pair_gain_hbm,
    pair_bias_hbm,
    qk_weight_hbm,
    qk_bias_hbm,
    pair_weight_hbm,
    bins_hbm,
    relpos_hbm,
    chain_hbm,
    chain_table_hbm,
    single_ref,
    pair_ref,
    base_ref,
    last_keys_ref,
    q_ref,
    weight_ref,
    hidden_v,
    mix_s,
    norm_v,
    proj_in_v,
    vec_v,
    proj_out_v,
    tokens_s,
    residue_table_v,
    qk_weight_v,
    qk_bias_v,
    pair_weight_v,
    bins_v,
    relpos_v,
    chain_s,
    chain_table_v,
    mixture_v,
    residue_v,
    tables_v,
    base_v,
    keys_v,
    send_sem,
    recv_sems,
):
    me = lax.axis_index("seq")
    barrier = pltpu.get_barrier_semaphore()
    nst, tok, d = hidden_v.shape
    inner = pair_weight_v.shape[0] // 2
    length = bins_v.shape[1]
    cz = pair_weight_v.shape[1]
    nbins = relpos_v.shape[0]
    nbins_pad = tables_v.shape[0] // 2
    per = n // parts
    width = per * tok
    first = length - width

    def group_of(source):
        return jnp.maximum(source - n // 2 + per, 0) // per

    def produce(copy_sems):
        n_sems = [0]

        def fetch(*pairs):
            sem = copy_sems.at[n_sems[0]]
            n_sems[0] += 1
            copies = [pltpu.make_async_copy(src, dst, sem) for src, dst in pairs]
            for copy in copies:
                copy.start()
            return copies[0]

        def whole(ref):
            sem = copy_sems.at[n_sems[0] - 1]
            return pltpu.make_async_copy(ref, ref, sem)

        mix_copy = fetch((mix_hbm, mix_s))
        h_width = d // h_chunks
        h_copies = [
            fetch(
                (
                    hidden_hbm.at[:, :, pl.ds(c * h_width, h_width)],
                    hidden_v.at[:, :, pl.ds(c * h_width, h_width)],
                )
            )
            for c in range(h_chunks)
        ]
        fetch((norm_gain_hbm, norm_v.at[0]), (norm_bias_hbm, norm_v.at[1]))
        norm_copy = whole(norm_v)
        k_depth = d // k_chunks
        tok_copy = fetch((tokens_hbm, tokens_s))
        chain_copy = fetch((chain_hbm, chain_s))
        table_copy = fetch((residue_table_hbm, residue_table_v))
        fetch(
            (proj_in_bias_hbm, vec_v.at[0]),
            (proj_out_bias_hbm, vec_v.at[1]),
            (pair_gain_hbm, vec_v.at[2]),
            (pair_bias_hbm, vec_v.at[3]),
        )
        vec_copy = whole(vec_v)
        qk_copies = [fetch((qk_weight_hbm, qk_weight_v)), fetch((qk_bias_hbm, qk_bias_v))]
        in_copies = [
            fetch(
                (
                    proj_in_hbm.at[pl.ds(c * k_depth, k_depth), :],
                    proj_in_v.at[pl.ds(c * k_depth, k_depth), :],
                )
            )
            for c in range(k_chunks)
        ]
        o_depth = proj_out_v.shape[0] // o_chunks
        out_copies = [
            fetch(
                (
                    proj_out_hbm.at[pl.ds(c * o_depth, o_depth), :],
                    proj_out_v.at[pl.ds(c * o_depth, o_depth), :],
                )
            )
            for c in range(o_chunks)
        ]

        for step in range(1, n):
            pl.semaphore_signal(
                barrier,
                inc=1,
                device_id={"seq": lax.rem(me + step, n)},
                device_id_type=MESH,
            )

        mix_copy.wait()
        for c in range(h_chunks):
            h_copies[c].wait()
            cols = pl.ds(c * h_width, h_width)
            total = mix_s[0] * hidden_v[0, :, cols].astype(F32)
            for k in range(1, nst):
                total = total + mix_s[k] * hidden_v[k, :, cols].astype(F32)
            mixture_v[:, cols] = total

        norm_copy.wait()
        normed = layer_norm(mixture_v[...], as_row(norm_v[0]), as_row(norm_v[1])).astype(BF16)

        hidden = jnp.zeros((tok, proj_in_v.shape[1]), F32)
        for c in range(k_chunks):
            in_copies[c].wait()
            hidden = hidden + jnp.dot(
                normed[:, c * k_depth : (c + 1) * k_depth],
                proj_in_v[pl.ds(c * k_depth, k_depth), :],
                preferred_element_type=F32,
            )
            if c == 0:
                tok_copy.wait()
                chain_copy.wait()
                table_copy.wait()
                for i in range(tok):
                    residue_v[pl.ds(i, 1), :] = residue_table_v[pl.ds(tokens_s[i], 1), :]
                span = (LANES - inner) // 2
                lane = lax.broadcasted_iota(jnp.int32, (tok, LANES), 1)
                chains = column_of(chain_s, tok, (tok, LANES))
                onehot = jnp.where(
                    (lane == chains + inner) | (lane == chains + (inner + span)), 1.0, 0.0
                ).astype(F32)
            if c == min(1, k_chunks - 1):
                vec_copy.wait()
                for copy in qk_copies:
                    copy.wait()
                gain = vec_v[2]
                qk_weight = qk_weight_v[...]
                affine = sum_three(
                    jnp.dot(
                        split_three(
                            jnp.concatenate(
                                [jnp.broadcast_to(gain, (8,) + gain.shape[1:]), jnp.broadcast_to(vec_v[3], (8,) + gain.shape[1:])],
                                axis=0,
                            )
                        ),
                        qk_weight,
                        preferred_element_type=F32,
                    )
                )
                gain_w = affine[0:1]
                bias_w = affine[8:9] + qk_bias_v[...]
        hidden = jnp.maximum(hidden + vec_v[0], 0.0).astype(BF16)
        single_f = vec_v[1] + residue_v[...]
        for c in range(o_chunks):
            out_copies[c].wait()
            single_f = single_f + jnp.dot(
                hidden[:, c * o_depth : (c + 1) * o_depth],
                proj_out_v[pl.ds(c * o_depth, o_depth), :],
                preferred_element_type=F32,
            )
        raw = jnp.dot(split_rows(single_f * gain), qk_weight, preferred_element_type=F32)
        mean = jnp.mean(single_f, axis=-1, keepdims=True)
        center = single_f - mean
        scale = lax.rsqrt(jnp.mean(center * center, axis=-1, keepdims=True) + epsilon)
        query_key = (raw[:tok] + raw[tok:] - mean * gain_w) * scale + bias_w

        q_rows = jnp.where(lane < inner, query_key, onehot).astype(BF16)
        keys_v[me] = jnp.where(
            lane < inner, pltpu.roll(query_key, LANES - inner, 1), onehot
        ).astype(BF16)

        pl.semaphore_wait(barrier, n - 1)
        for place in range(n):
            target = jnp.where(2 * me >= n, place, n - 1 - place)

            @pl.when(target != me)
            def _():
                pltpu.make_async_remote_copy(
                    src_ref=keys_v.at[me],
                    dst_ref=keys_v.at[me],
                    send_sem=send_sem,
                    recv_sem=recv_sems.at[group_of(me)],
                    device_id={"seq": target},
                    device_id_type=MESH,
                ).start()

        pair_copies = [
            fetch((pair_weight_hbm, pair_weight_v)),
            fetch((bins_hbm, bins_v)),
            fetch((relpos_hbm, relpos_v)),
            fetch((chain_table_hbm, chain_table_v)),
        ]
        q_ref[...] = q_rows
        single_ref[...] = single_f.astype(BF16)
        for copy in pair_copies:
            copy.wait()
        pair_weight = pair_weight_v[...]
        low_weight = pair_weight[inner:]
        row_diff = jnp.dot(q_rows[:, :inner], low_weight, preferred_element_type=F32)
        chain_base = chain_table_v[pl.ds(0, 1), :]
        chain_hi, chain_lo = split_hi_lo(chain_table_v[pl.ds(1, 1), :] - chain_base)
        weight = jnp.concatenate(
            [
                pair_weight[:inner],
                jnp.broadcast_to(chain_hi, (span, cz)),
                jnp.broadcast_to(chain_lo, (span, cz)),
                -low_weight,
                jnp.zeros((LANES - inner, cz), BF16),
            ],
            axis=0,
        )
        weight_ref[...] = weight
        tables_v[...] = jnp.zeros_like(tables_v)
        hi, lo = split_hi_lo(relpos_v[...])
        tables_v[pl.ds(0, nbins), :] = hi
        tables_v[pl.ds(nbins_pad, nbins), :] = lo
        tables = tables_v[...]
        row_base = row_diff + chain_base
        bins = jnp.concatenate(
            [bins_v[...], jnp.zeros((LANES - tok, length), jnp.int32)], axis=0
        )
        bins_t = bins.T
        bin_lane = lax.broadcasted_iota(jnp.int32, (length, nbins_pad), 1)
        for i in range(tok):
            hot = jnp.where(bins_t[:, i : i + 1] == bin_lane, 1.0, 0.0).astype(BF16)
            base = (
                jnp.dot(
                    jnp.concatenate([hot, hot], axis=1), tables, preferred_element_type=F32
                )
                + row_base[i : i + 1]
            )
            base_v[i] = base[:first]
            base_ref[i] = base[first:]

    pl.run_scoped(produce, pltpu.SemaphoreType.DMA((n_copies,)))
    q_rows = q_ref[...]
    weight = weight_ref[...]

    def arrived(group, count):
        block = keys_v.at[pl.ds(0, count)]
        pltpu.make_async_remote_copy(
            src_ref=block,
            dst_ref=block,
            send_sem=send_sem,
            recv_sem=recv_sems.at[group],
            device_id={"seq": lax.rem(me + 1, n)},
            device_id_type=MESH,
        ).wait_recv()

    for part in range(parts):
        if part == 0 or part >= parts // 2:
            group = max(0, part - parts // 2 + 1)
            count = n // 2 if part == 0 else per
            own = group_of(me) == group

            @pl.when(jnp.logical_not(own))
            def _():
                arrived(group, count)

            if count > 1:

                @pl.when(own)
                def _():
                    arrived(group, count - 1)

        keys = keys_v[pl.ds(part * per, per)].reshape(width, LANES)
        if part == parts - 1:
            last_keys_ref[...] = keys
        else:
            block = pair_block(keys, q_rows, weight, range(tok))
            for i in range(tok):
                pair_ref[i, pl.ds(part * width, width), :] = (
                    block[i * width : (i + 1) * width]
                    + base_v[i, pl.ds(part * width, width), :]
                ).astype(BF16)
    sent = keys_v.at[pl.ds(0, n - 1)]
    pltpu.make_async_remote_copy(
        src_ref=sent,
        dst_ref=sent,
        send_sem=send_sem,
        recv_sem=recv_sems.at[0],
        device_id={"seq": lax.rem(me + 1, n)},
        device_id_type=MESH,
    ).wait_send()


def finish(
    single_ref, pair_ref, base_ref, keys_ref, q_ref, weight_ref,
    single_hbm, pair_hbm, last_v, sems,
):
    tok, width, cz = base_ref.shape
    first = pair_ref.shape[1]
    copies = []

    def put(src, dst):
        copies.append(pltpu.make_async_copy(src, dst, sems.at[len(copies)]))
        copies[-1].start()

    put(pair_ref, pair_hbm.at[:, pl.ds(0, first), :])
    put(single_ref, single_hbm)
    halves = 2
    rows = tok // halves
    for h in range(halves):
        block = pair_block(
            keys_ref[...], q_ref[...], weight_ref[...], range(h * rows, (h + 1) * rows)
        )
        for i in range(rows):
            last_v[h * rows + i] = (
                block[i * width : (i + 1) * width] + base_ref[h * rows + i]
            ).astype(BF16)
        put(
            last_v.at[pl.ds(h * rows, rows)],
            pair_hbm.at[pl.ds(h * rows, rows), pl.ds(first, width), :],
        )
    for copy in copies:
        copy.wait()


def shards(n, *args):
    (hidden, mix, norm_gain, norm_bias, proj_in, proj_in_bias, proj_out, proj_out_bias,
     tokens, residue_table, pair_gain, pair_bias, qk_weight, qk_bias, pair_weight,
     bins, relpos, chain, chain_table) = args
    row = lambda a: a.reshape(1, a.shape[0])
    tiles = lambda a: a.reshape(a.shape[0] // LANES, LANES)
    args = (hidden, mix, tiles(norm_gain), tiles(norm_bias), proj_in, row(proj_in_bias),
            proj_out, row(proj_out_bias), tokens, residue_table, row(pair_gain),
            row(pair_bias), qk_weight, row(qk_bias), pair_weight, bins, relpos, chain,
            chain_table)
    args = tuple(pltpu.with_memory_space_constraint(a, pltpu.HBM) for a in args)
    nst, tok, d = hidden.shape
    cs = proj_out.shape[1]
    cz = pair_weight.shape[1]
    length = bins.shape[1]
    like = lambda a: pltpu.VMEM(a.shape, a.dtype)
    scalars = lambda a: pltpu.SMEM(a.shape, a.dtype)
    nbins_pad = -(-relpos.shape[0] // LANES) * LANES
    h_chunks, k_chunks = (5, 10) if d % (10 * LANES) == 0 else (1, 1)
    o_chunks = 4 if proj_out.shape[0] % (4 * LANES) == 0 else 1
    n_copies = 14 + h_chunks + k_chunks + o_chunks
    parts = 8 if n % 8 == 0 else 2
    width = length // parts
    first = length - width
    vmem = pl.BlockSpec(memory_space=pltpu.VMEM)
    hbm = pl.BlockSpec(memory_space=pltpu.HBM)
    mid = pl.pallas_call(
        functools.partial(kernel, n, parts, h_chunks, k_chunks, o_chunks, n_copies),
        out_shape=(
            jax.ShapeDtypeStruct((tok, cs), BF16),
            jax.ShapeDtypeStruct((tok, first, cz), BF16),
            jax.ShapeDtypeStruct((tok, width, cz), F32),
            jax.ShapeDtypeStruct((width, LANES), BF16),
            jax.ShapeDtypeStruct((tok, LANES), BF16),
            jax.ShapeDtypeStruct((2 * LANES, cz), BF16),
        ),
        in_specs=[hbm] * len(args),
        out_specs=(vmem,) * 6,
        scratch_shapes=[
            like(hidden),
            scalars(mix),
            pltpu.VMEM((2, d // LANES, LANES), F32),
            like(proj_in),
            pltpu.VMEM((4, 1, cs), F32),
            like(proj_out),
            scalars(tokens),
            like(residue_table),
            like(qk_weight),
            pltpu.VMEM((1, qk_bias.shape[0]), F32),
            like(pair_weight),
            like(bins),
            like(relpos),
            scalars(chain),
            like(chain_table),
            pltpu.VMEM((tok, d), F32),
            pltpu.VMEM((tok, cs), F32),
            pltpu.VMEM((2 * nbins_pad, cz), BF16),
            pltpu.VMEM((tok, first, cz), F32),
            pltpu.VMEM((n, tok, LANES), BF16),
            pltpu.SemaphoreType.DMA,
            pltpu.SemaphoreType.DMA((parts // 2 + 1,)),
        ],
        compiler_params=pltpu.CompilerParams(
            collective_id=0, has_side_effects=True, vmem_limit_bytes=40 << 20
        ),
    )(*args)
    return pl.pallas_call(
        finish,
        out_shape=(
            jax.ShapeDtypeStruct((tok, cs), BF16),
            jax.ShapeDtypeStruct((tok, length, cz), BF16),
        ),
        in_specs=[vmem] * 6,
        out_specs=(hbm, hbm),
        scratch_shapes=[
            pltpu.VMEM((tok, width, cz), BF16),
            pltpu.SemaphoreType.DMA((4,)),
        ],
        compiler_params=pltpu.CompilerParams(vmem_limit_bytes=16 << 20),
    )(*mid)


def solution(mesh):
    in_specs = (
        P(None, ("groups", "seq"), None),
        P(),
        P(),
        P(),
        P(),
        P(),
        P(),
        P(),
        P(("groups", "seq")),
        P(),
        P(),
        P(),
        P(),
        P(),
        P(),
        P(("groups", "seq"), None),
        P(),
        P(("groups", "seq")),
        P(),
    )
    out_specs = (P(("groups", "seq"), None), P(("groups", "seq"), None, None))
    return jax.shard_map(
        functools.partial(shards, mesh.shape["seq"]),
        mesh=mesh,
        in_specs=in_specs,
        out_specs=out_specs,
        check_vma=False,
    )
```

```python
import functools

import jax
import jax.numpy as jnp
from jax import lax
from jax.experimental import pallas as pl
from jax.experimental.pallas import tpu as pltpu
from jax.sharding import PartitionSpec as P

epsilon = 1e-05
F32 = jnp.float32
BF16 = jnp.bfloat16
LANES = 128
MESH = pl.DeviceIdType.MESH


def layer_norm(values, weight_gain, weight_bias):
    center = values - jnp.mean(values, axis=-1, keepdims=True)
    spread = jnp.mean(center * center, axis=-1, keepdims=True)
    return center * lax.rsqrt(spread + epsilon) * weight_gain + weight_bias


def split_hi_lo(values):
    hi = values.astype(BF16)
    lo = (values - hi.astype(F32)).astype(BF16)
    return hi, lo


def split_three(values):
    hi = values.astype(BF16)
    rest = values - hi.astype(F32)
    mid = rest.astype(BF16)
    low = (rest - mid.astype(F32)).astype(BF16)
    return jnp.concatenate([hi, mid, low], axis=0)


def split_rows(values):
    return jnp.concatenate(split_hi_lo(values), axis=0)


def sum_three(stacked):
    rows = stacked.shape[0] // 3
    return stacked[:rows] + (stacked[rows : 2 * rows] + stacked[2 * rows :])


def column_of(scalars_ref, count, shape):
    rows = lax.broadcasted_iota(jnp.int32, shape, 0)
    out = jnp.zeros(shape, jnp.int32)
    for i in range(count):
        out = jnp.where(rows == i, scalars_ref[i], out)
    return out


def as_row(tiles):
    return jnp.concatenate([tiles[r : r + 1] for r in range(tiles.shape[0])], axis=1)


def pair_block(keys, q_rows, weight, rows):
    lhs = [jnp.concatenate([keys * q_rows[i : i + 1], keys], axis=1) for i in rows]
    return jnp.dot(jnp.concatenate(lhs, axis=0), weight, preferred_element_type=F32)


def kernel(
    n,
    parts,
    h_chunks,
    k_chunks,
    o_chunks,
    n_copies,
    hidden_hbm,
    mix_hbm,
    norm_gain_hbm,
    norm_bias_hbm,
    proj_in_hbm,
    proj_in_bias_hbm,
    proj_out_hbm,
    proj_out_bias_hbm,
    tokens_hbm,
    residue_table_hbm,
    pair_gain_hbm,
    pair_bias_hbm,
    qk_weight_hbm,
    qk_bias_hbm,
    pair_weight_hbm,
    bins_hbm,
    relpos_hbm,
    chain_hbm,
    chain_table_hbm,
    single_ref,
    pair_ref,
    base_ref,
    last_keys_ref,
    q_ref,
    weight_ref,
    hidden_v,
    mix_s,
    norm_v,
    proj_in_v,
    vec_v,
    proj_out_v,
    tokens_s,
    residue_table_v,
    qk_weight_v,
    qk_bias_v,
    pair_weight_v,
    bins_v,
    relpos_v,
    chain_s,
    chain_table_v,
    mixture_v,
    residue_v,
    tables_v,
    base_v,
    keys_v,
    send_sem,
    recv_sems,
):
    me = lax.axis_index("seq")
    barrier = pltpu.get_barrier_semaphore()
    nst, tok, d = hidden_v.shape
    inner = pair_weight_v.shape[0] // 2
    length = bins_v.shape[1]
    cz = pair_weight_v.shape[1]
    nbins = relpos_v.shape[0]
    nbins_pad = tables_v.shape[0] // 2
    per = n // parts
    width = per * tok
    first = length - width

    def group_of(source):
        return jnp.maximum(source - n // 2 + per, 0) // per

    def produce(copy_sems):
        n_sems = [0]

        def fetch(*pairs):
            sem = copy_sems.at[n_sems[0]]
            n_sems[0] += 1
            copies = [pltpu.make_async_copy(src, dst, sem) for src, dst in pairs]
            for copy in copies:
                copy.start()
            return copies[0]

        def whole(ref):
            sem = copy_sems.at[n_sems[0] - 1]
            return pltpu.make_async_copy(ref, ref, sem)

        mix_copy = fetch((mix_hbm, mix_s))
        h_width = d // h_chunks
        h_copies = [
            fetch(
                (
                    hidden_hbm.at[:, :, pl.ds(c * h_width, h_width)],
                    hidden_v.at[:, :, pl.ds(c * h_width, h_width)],
                )
            )
            for c in range(h_chunks)
        ]
        fetch((norm_gain_hbm, norm_v.at[0]), (norm_bias_hbm, norm_v.at[1]))
        norm_copy = whole(norm_v)
        k_depth = d // k_chunks
        tok_copy = fetch((tokens_hbm, tokens_s))
        chain_copy = fetch((chain_hbm, chain_s))
        table_copy = fetch((residue_table_hbm, residue_table_v))
        fetch(
            (proj_in_bias_hbm, vec_v.at[0]),
            (proj_out_bias_hbm, vec_v.at[1]),
            (pair_gain_hbm, vec_v.at[2]),
            (pair_bias_hbm, vec_v.at[3]),
        )
        vec_copy = whole(vec_v)
        qk_copies = [fetch((qk_weight_hbm, qk_weight_v)), fetch((qk_bias_hbm, qk_bias_v))]
        in_copies = [
            fetch(
                (
                    proj_in_hbm.at[pl.ds(c * k_depth, k_depth), :],
                    proj_in_v.at[pl.ds(c * k_depth, k_depth), :],
                )
            )
            for c in range(k_chunks)
        ]
        o_depth = proj_out_v.shape[0] // o_chunks
        out_copies = [
            fetch(
                (
                    proj_out_hbm.at[pl.ds(c * o_depth, o_depth), :],
                    proj_out_v.at[pl.ds(c * o_depth, o_depth), :],
                )
            )
            for c in range(o_chunks)
        ]

        for step in range(1, n):
            pl.semaphore_signal(
                barrier,
                inc=1,
                device_id={"seq": lax.rem(me + step, n)},
                device_id_type=MESH,
            )

        mix_copy.wait()
        for c in range(h_chunks):
            h_copies[c].wait()
            cols = pl.ds(c * h_width, h_width)
            total = mix_s[0] * hidden_v[0, :, cols].astype(F32)
            for k in range(1, nst):
                total = total + mix_s[k] * hidden_v[k, :, cols].astype(F32)
            mixture_v[:, cols] = total

        norm_copy.wait()
        normed = layer_norm(mixture_v[...], as_row(norm_v[0]), as_row(norm_v[1])).astype(BF16)

        hidden = jnp.zeros((tok, proj_in_v.shape[1]), F32)
        for c in range(k_chunks):
            in_copies[c].wait()
            hidden = hidden + jnp.dot(
                normed[:, c * k_depth : (c + 1) * k_depth],
                proj_in_v[pl.ds(c * k_depth, k_depth), :],
                preferred_element_type=F32,
            )
            if c == 0:
                tok_copy.wait()
                chain_copy.wait()
                table_copy.wait()
                for i in range(tok):
                    residue_v[pl.ds(i, 1), :] = residue_table_v[pl.ds(tokens_s[i], 1), :]
                span = (LANES - inner) // 2
                lane = lax.broadcasted_iota(jnp.int32, (tok, LANES), 1)
                chains = column_of(chain_s, tok, (tok, LANES))
                onehot = jnp.where(
                    (lane == chains + inner) | (lane == chains + (inner + span)), 1.0, 0.0
                ).astype(F32)
            if c == min(1, k_chunks - 1):
                vec_copy.wait()
                for copy in qk_copies:
                    copy.wait()
                gain = vec_v[2]
                qk_weight = qk_weight_v[...]
                affine = sum_three(
                    jnp.dot(
                        split_three(
                            jnp.concatenate(
                                [jnp.broadcast_to(gain, (8,) + gain.shape[1:]), jnp.broadcast_to(vec_v[3], (8,) + gain.shape[1:])],
                                axis=0,
                            )
                        ),
                        qk_weight,
                        preferred_element_type=F32,
                    )
                )
                gain_w = affine[0:1]
                bias_w = affine[8:9] + qk_bias_v[...]
        hidden = jnp.maximum(hidden + vec_v[0], 0.0).astype(BF16)
        single_f = vec_v[1] + residue_v[...]
        for c in range(o_chunks):
            if c == o_chunks - 1:
                pl.semaphore_wait(barrier, n - 1)
            out_copies[c].wait()
            single_f = single_f + jnp.dot(
                hidden[:, c * o_depth : (c + 1) * o_depth],
                proj_out_v[pl.ds(c * o_depth, o_depth), :],
                preferred_element_type=F32,
            )
        raw = jnp.dot(split_rows(single_f * gain), qk_weight, preferred_element_type=F32)
        mean = jnp.mean(single_f, axis=-1, keepdims=True)
        center = single_f - mean
        scale = lax.rsqrt(jnp.mean(center * center, axis=-1, keepdims=True) + epsilon)
        query_key = (raw[:tok] + raw[tok:] - mean * gain_w) * scale + bias_w

        q_rows = jnp.where(lane < inner, query_key, onehot).astype(BF16)
        keys_v[me] = jnp.where(
            lane < inner, pltpu.roll(query_key, LANES - inner, 1), onehot
        ).astype(BF16)

        for place in range(n):
            target = jnp.where(2 * me >= n, place, n - 1 - place)

            @pl.when(target != me)
            def _():
                pltpu.make_async_remote_copy(
                    src_ref=keys_v.at[me],
                    dst_ref=keys_v.at[me],
                    send_sem=send_sem,
                    recv_sem=recv_sems.at[group_of(me)],
                    device_id={"seq": target},
                    device_id_type=MESH,
                ).start()

        pair_copies = [
            fetch((pair_weight_hbm, pair_weight_v)),
            fetch((bins_hbm, bins_v)),
            fetch((relpos_hbm, relpos_v)),
            fetch((chain_table_hbm, chain_table_v)),
        ]
        q_ref[...] = q_rows
        single_ref[...] = single_f.astype(BF16)
        for copy in pair_copies:
            copy.wait()
        pair_weight = pair_weight_v[...]
        low_weight = pair_weight[inner:]
        row_diff = jnp.dot(q_rows[:, :inner], low_weight, preferred_element_type=F32)
        chain_base = chain_table_v[pl.ds(0, 1), :]
        chain_hi, chain_lo = split_hi_lo(chain_table_v[pl.ds(1, 1), :] - chain_base)
        weight = jnp.concatenate(
            [
                pair_weight[:inner],
                jnp.broadcast_to(chain_hi, (span, cz)),
                jnp.broadcast_to(chain_lo, (span, cz)),
                -low_weight,
                jnp.zeros((LANES - inner, cz), BF16),
            ],
            axis=0,
        )
        weight_ref[...] = weight
        tables_v[...] = jnp.zeros_like(tables_v)
        hi, lo = split_hi_lo(relpos_v[...])
        tables_v[pl.ds(0, nbins), :] = hi
        tables_v[pl.ds(nbins_pad, nbins), :] = lo
        tables = tables_v[...]
        row_base = row_diff + chain_base
        bins = jnp.concatenate(
            [bins_v[...], jnp.zeros((LANES - tok, length), jnp.int32)], axis=0
        )
        bins_t = bins.T
        bin_lane = lax.broadcasted_iota(jnp.int32, (length, nbins_pad), 1)
        for i in range(tok):
            hot = jnp.where(bins_t[:, i : i + 1] == bin_lane, 1.0, 0.0).astype(BF16)
            base = (
                jnp.dot(
                    jnp.concatenate([hot, hot], axis=1), tables, preferred_element_type=F32
                )
                + row_base[i : i + 1]
            )
            base_v[i] = base[:first]
            base_ref[i] = base[first:]

    pl.run_scoped(produce, pltpu.SemaphoreType.DMA((n_copies,)))
    q_rows = q_ref[...]
    weight = weight_ref[...]

    def arrived(group, count):
        block = keys_v.at[pl.ds(0, count)]
        pltpu.make_async_remote_copy(
            src_ref=block,
            dst_ref=block,
            send_sem=send_sem,
            recv_sem=recv_sems.at[group],
            device_id={"seq": lax.rem(me + 1, n)},
            device_id_type=MESH,
        ).wait_recv()

    for part in range(parts):
        if part == 0 or part >= parts // 2:
            group = max(0, part - parts // 2 + 1)
            count = n // 2 if part == 0 else per
            own = group_of(me) == group

            @pl.when(jnp.logical_not(own))
            def _():
                arrived(group, count)

            if count > 1:

                @pl.when(own)
                def _():
                    arrived(group, count - 1)

        keys = keys_v[pl.ds(part * per, per)].reshape(width, LANES)
        if part == parts - 1:
            last_keys_ref[...] = keys
        else:
            block = pair_block(keys, q_rows, weight, range(tok))
            for i in range(tok):
                pair_ref[i, pl.ds(part * width, width), :] = (
                    block[i * width : (i + 1) * width]
                    + base_v[i, pl.ds(part * width, width), :]
                ).astype(BF16)
    sent = keys_v.at[pl.ds(0, n - 1)]
    pltpu.make_async_remote_copy(
        src_ref=sent,
        dst_ref=sent,
        send_sem=send_sem,
        recv_sem=recv_sems.at[0],
        device_id={"seq": lax.rem(me + 1, n)},
        device_id_type=MESH,
    ).wait_send()


def finish(
    single_ref, pair_ref, base_ref, keys_ref, q_ref, weight_ref,
    single_hbm, pair_hbm, last_v, sems,
):
    tok, width, cz = base_ref.shape
    first = pair_ref.shape[1]
    copies = []

    def put(src, dst):
        copies.append(pltpu.make_async_copy(src, dst, sems.at[len(copies)]))
        copies[-1].start()

    put(pair_ref, pair_hbm.at[:, pl.ds(0, first), :])
    put(single_ref, single_hbm)
    halves = 2
    rows = tok // halves
    for h in range(halves):
        block = pair_block(
            keys_ref[...], q_ref[...], weight_ref[...], range(h * rows, (h + 1) * rows)
        )
        for i in range(rows):
            last_v[h * rows + i] = (
                block[i * width : (i + 1) * width] + base_ref[h * rows + i]
            ).astype(BF16)
        put(
            last_v.at[pl.ds(h * rows, rows)],
            pair_hbm.at[pl.ds(h * rows, rows), pl.ds(first, width), :],
        )
    for copy in copies:
        copy.wait()


def shards(n, *args):
    (hidden, mix, norm_gain, norm_bias, proj_in, proj_in_bias, proj_out, proj_out_bias,
     tokens, residue_table, pair_gain, pair_bias, qk_weight, qk_bias, pair_weight,
     bins, relpos, chain, chain_table) = args
    row = lambda a: a.reshape(1, a.shape[0])
    tiles = lambda a: a.reshape(a.shape[0] // LANES, LANES)
    args = (hidden, mix, tiles(norm_gain), tiles(norm_bias), proj_in, row(proj_in_bias),
            proj_out, row(proj_out_bias), tokens, residue_table, row(pair_gain),
            row(pair_bias), qk_weight, row(qk_bias), pair_weight, bins, relpos, chain,
            chain_table)
    args = tuple(pltpu.with_memory_space_constraint(a, pltpu.HBM) for a in args)
    nst, tok, d = hidden.shape
    cs = proj_out.shape[1]
    cz = pair_weight.shape[1]
    length = bins.shape[1]
    like = lambda a: pltpu.VMEM(a.shape, a.dtype)
    scalars = lambda a: pltpu.SMEM(a.shape, a.dtype)
    nbins_pad = -(-relpos.shape[0] // LANES) * LANES
    h_chunks, k_chunks = (5, 10) if d % (10 * LANES) == 0 else (1, 1)
    o_chunks = 4 if proj_out.shape[0] % (4 * LANES) == 0 else 1
    n_copies = 14 + h_chunks + k_chunks + o_chunks
    parts = 8 if n % 8 == 0 else 2
    width = length // parts
    first = length - width
    vmem = pl.BlockSpec(memory_space=pltpu.VMEM)
    hbm = pl.BlockSpec(memory_space=pltpu.HBM)
    mid = pl.pallas_call(
        functools.partial(kernel, n, parts, h_chunks, k_chunks, o_chunks, n_copies),
        out_shape=(
            jax.ShapeDtypeStruct((tok, cs), BF16),
            jax.ShapeDtypeStruct((tok, first, cz), BF16),
            jax.ShapeDtypeStruct((tok, width, cz), F32),
            jax.ShapeDtypeStruct((width, LANES), BF16),
            jax.ShapeDtypeStruct((tok, LANES), BF16),
            jax.ShapeDtypeStruct((2 * LANES, cz), BF16),
        ),
        in_specs=[hbm] * len(args),
        out_specs=(vmem,) * 6,
        scratch_shapes=[
            like(hidden),
            scalars(mix),
            pltpu.VMEM((2, d // LANES, LANES), F32),
            like(proj_in),
            pltpu.VMEM((4, 1, cs), F32),
            like(proj_out),
            scalars(tokens),
            like(residue_table),
            like(qk_weight),
            pltpu.VMEM((1, qk_bias.shape[0]), F32),
            like(pair_weight),
            like(bins),
            like(relpos),
            scalars(chain),
            like(chain_table),
            pltpu.VMEM((tok, d), F32),
            pltpu.VMEM((tok, cs), F32),
            pltpu.VMEM((2 * nbins_pad, cz), BF16),
            pltpu.VMEM((tok, first, cz), F32),
            pltpu.VMEM((n, tok, LANES), BF16),
            pltpu.SemaphoreType.DMA,
            pltpu.SemaphoreType.DMA((parts // 2 + 1,)),
        ],
        compiler_params=pltpu.CompilerParams(
            collective_id=0, has_side_effects=True, vmem_limit_bytes=40 << 20
        ),
    )(*args)
    return pl.pallas_call(
        finish,
        out_shape=(
            jax.ShapeDtypeStruct((tok, cs), BF16),
            jax.ShapeDtypeStruct((tok, length, cz), BF16),
        ),
        in_specs=[vmem] * 6,
        out_specs=(hbm, hbm),
        scratch_shapes=[
            pltpu.VMEM((tok, width, cz), BF16),
            pltpu.SemaphoreType.DMA((4,)),
        ],
        compiler_params=pltpu.CompilerParams(vmem_limit_bytes=16 << 20),
    )(*mid)


def solution(mesh):
    in_specs = (
        P(None, ("groups", "seq"), None),
        P(),
        P(),
        P(),
        P(),
        P(),
        P(),
        P(),
        P(("groups", "seq")),
        P(),
        P(),
        P(),
        P(),
        P(),
        P(),
        P(("groups", "seq"), None),
        P(),
        P(("groups", "seq")),
        P(),
    )
    out_specs = (P(("groups", "seq"), None), P(("groups", "seq"), None, None))
    return jax.shard_map(
        functools.partial(shards, mesh.shape["seq"]),
        mesh=mesh,
        in_specs=in_specs,
        out_specs=out_specs,
        check_vma=False,
    )
```
